32 devices in a mesh: pb: 8 (over y, x, core), row: 4 (over z).
Axes of the slice: x: 2, y: 2, z: 4, core: 2. Of those that a mesh axis runs over, the one named last changes fastest.
Arguments:
- valence_bands: bfloat16 [8, 20, 4096], P('pb', None, 'row'), may hold values from -0.75 to 0.75
- conduction_bands: bfloat16 [8, 20, 4096], P('pb', None, 'row'), may hold values from -6 to 6
- screened: bfloat16 [8, 4096, 4096], P('pb', 'row'), may hold values from -0.09375 to 0.09375
- pair_list: int32 [16, 2], replicated, may hold values from 0 to 7, as said below
- transfer_index: int32 [16, 1], replicated, may hold values from 0 to 7; in each aligned block of 16 rows (0 to 15, 16 to 31, ...) at most 6 rows name the same one
- owner_map: int32 [8], replicated, may hold values from 0 to 7, as said below
Outputs:
- direct: bfloat16 [16, 400, 400], P('pb', 'row')
- mirror: bfloat16 [16, 400, 400], P('pb', 'row')
The draws below stay inside these ranges and needn't reach their ends.
Inputs may be any that keep to these rules, and one draw needn't show every extreme that they name: owner_map is a permutation of 0 to 7. `pair_list`: the two k-points of a pair differ. The first k-point of pairs e * 2 to e * 2 + 1 is the one that owner_map sends to e. Over all pairs, the second k-points are sent by owner_map to every value 0 to 7 exactly 2 times. `transfer_index`: at most 6 pairs share one momentum transfer, and some transfer has exactly 6; every transfer has at least one pair.
All inputs are finite; a program needn't handle non-finite values.
Results may differ from the reference program's by a relative error of at most 0.0065.
Values may be sent and summed in bfloat16 or wider, within the bound.
No kernel may reach another device: no remote copies, remote signals or barrier semaphores. Data moves between devices by JAX's collectives and lax.ppermute only.
A program may use at most 64 MiB of HBM per device.

```python
import math
import jax
import jax.numpy as jnp
import numpy as np
from jax import lax

NMU = 4096
NV = 20
NC = 20
PAIR_DEV = 2
MOST = 6
NK = 8
NQ = 8
NPAIRS = 16
N_PB = 8


def pair_layout(key):
    owner_map = jax.random.permutation(jax.random.fold_in(key, 71), NK).astype(jnp.int32)
    holder = jnp.argsort(owner_map).astype(jnp.int32)
    columns = []
    for repeat in range(PAIR_DEV):
        shuffle = jax.random.permutation(jax.random.fold_in(key, 100 + repeat), NK).astype(jnp.int32)
        inverse = jnp.argsort(shuffle).astype(jnp.int32)
        offset = jax.random.randint(jax.random.fold_in(key, 300 + repeat), (), 1, NK).astype(jnp.int32)
        partner = inverse[(shuffle + offset) % NK]
        columns.append(jnp.stack([holder, holder[partner]], axis=1))
    pair_list = jnp.stack(columns, axis=1).reshape(NK * PAIR_DEV, 2).astype(jnp.int32)
    return (owner_map, pair_list)


def draw_pair_list(key, part):
    return pair_layout(key)[1]


def draw_owner_map(key, part):
    return pair_layout(key)[0]


def shard_levels(rng, shape, shards, smallest, largest):
    def one(axis_at, shards_of):
        heights = jax.random.uniform(jax.random.fold_in(jax.random.fold_in(rng, 6), axis_at), (shards_of,), jnp.float32, smallest / len(shards), largest / len(shards))
        return jnp.repeat(jnp.exp(heights), shape[axis_at] // shards_of).reshape((-1,) + (1,) * (len(shape) - axis_at - 1))

    gain = one(*shards[0])
    for cut in shards[1:]:
        gain = gain * one(*cut)
    return gain


def deal_out(stream_key, own, number, rows, amount, top, most, slope):
    sequence = jax.random.permutation(stream_key, amount)
    heavy_load, ordinary = shares(amount, rows * top, most, slope, True), shares(amount, rows * top, most, slope, False)
    places = jnp.arange(amount)

    def named(sizes, offset_by):
        used = int((sizes > 0).sum())
        fixed = max(1, used // 4)
        moved = fixed + (places - fixed + offset_by * (used - fixed)) % max(1, amount - fixed)
        return jnp.zeros((amount,), jnp.int32).at[sequence[jnp.where(places < fixed, places, moved)]].set(jnp.asarray(sizes, jnp.int32))

    sizes = jnp.where(number % 4 == 0, named(heavy_load, number // 4), named(ordinary, number - number // 4 - 1))
    mixed = jax.random.permutation(jax.random.fold_in(own, 3), amount)
    giver, receiver = mixed[0:amount // 2 * 2:2], mixed[1:amount // 2 * 2:2]
    slack = jnp.minimum(sizes[giver] - 1, most - sizes[receiver]) // 2
    slack = jnp.where((giver == sequence[0]) | (receiver == sequence[0]) | (sizes[receiver] == 0), 0, jnp.maximum(slack, 0))
    moved = jax.random.randint(jax.random.fold_in(own, 4), (amount // 2,), 0, 1 << 20) % (slack + 1)
    sizes = sizes.at[giver].add(-moved).at[receiver].add(moved)
    members = jnp.searchsorted(jnp.cumsum(sizes), jnp.arange(rows * top), side="right").astype(jnp.int32)
    table = members.reshape(top, rows).T
    table = table[jax.random.permutation(jax.random.fold_in(own, 1), rows)]
    offset_by = jax.random.randint(jax.random.fold_in(own, 2), (rows, 1), 0, top)
    return jnp.take_along_axis(table, (jnp.arange(top)[None, :] + offset_by) % top, axis=1)


def shares(number_of, total, limit, skew, full):
    portions = [(1 << 20) // math.isqrt(standing ** skew) + 1 for standing in range(1, number_of + 1)]
    largest = limit if full else min(limit, max(-(-total // number_of), total * portions[0] // sum(portions)))
    least = 1 if total - largest >= number_of - 1 else 0
    counts, rest = [largest] + [least] * (number_of - 1), total - largest - least * (number_of - 1)
    while rest > 0:
        free = [i for i in range(1, number_of) if counts[i] < largest] or [i for i in range(1, number_of) if counts[i] < limit]
        mass, left = sum([portions[i] for i in free]), rest
        for i in free:
            extra = min(limit - counts[i], max(1, left * portions[i] // mass), rest)
            counts[i] = counts[i] + extra
            rest = rest - extra
    return np.array(counts)


def gaussian(key, dims, width, most, cuts=(), kind=jnp.bfloat16):
    result = width * jax.random.normal(key, dims, jnp.float32)
    if cuts:
        result = result * shard_levels(key, dims, cuts, -0.22, 0.18)
    return jnp.clip(result, -most, most).astype(kind)


def setup_inputs(seed: int = 0) -> dict:
    key_of = jax.random.split(jax.random.key(seed), 7)
    valence_bands = gaussian(key_of[0], (NK, NV, NMU), 0.125, 0.75, ((0, 8), (2, 4)))
    conduction_bands = gaussian(key_of[1], (NK, NC, NMU), 1.0, 6.0, ((0, 8), (2, 4)))
    screened = gaussian(key_of[2], (NQ, NMU, NMU), NMU ** -0.5, 0.09375, ((0, 8), (1, 4)))
    pair_list = draw_pair_list(jax.random.fold_in(key_of[6], 71), 0)
    transfer_index_keys = jax.random.split(jax.random.fold_in(key_of[4], 1), NPAIRS // NPAIRS)
    transfer_index_turns = jax.random.permutation(jax.random.fold_in(key_of[4], 3), NPAIRS // NPAIRS)
    transfer_index = jax.vmap(lambda own, number: deal_out(jax.random.fold_in(key_of[4], 2), own, number, NPAIRS, NQ, 1, MOST, 2))(transfer_index_keys, transfer_index_turns).reshape((NPAIRS, 1))
    owner_map = draw_owner_map(jax.random.fold_in(key_of[6], 71), 0)
    return dict(valence_bands=valence_bands, conduction_bands=conduction_bands, screened=screened, pair_list=pair_list, transfer_index=transfer_index, owner_map=owner_map)


def rank_table(labels, groups, slots_per):
    total_rows = labels.shape[0]
    member = (labels[None, :] == jnp.arange(groups, dtype=jnp.int32)[:, None]).astype(jnp.int32)
    before = jnp.cumsum(member, axis=1) - 1
    placed = member[:, None, :] * (before[:, None, :] == jnp.arange(slots_per, dtype=jnp.int32)[None, :, None]).astype(jnp.int32)
    numbers = jnp.arange(total_rows, dtype=jnp.int32) + 1
    return (jnp.sum(placed * numbers[None, None, :], axis=2) - 1).astype(jnp.int32)


def pair_kernel(val_first, val_second, con_first, con_second, screen_rows):
    val_count = val_first.shape[0]
    con_count = con_first.shape[0]
    val_pairs = (val_first[:, None, :].astype(jnp.float32) * val_second[None, :, :].astype(jnp.float32))
    val_pairs = val_pairs.reshape(val_count * val_count, val_first.shape[1]).astype(jnp.bfloat16)
    con_pairs = (con_first[:, None, :].astype(jnp.float32) * con_second[None, :, :].astype(jnp.float32))
    con_pairs = con_pairs.reshape(con_count * con_count, con_first.shape[1]).astype(jnp.bfloat16)
    interim = lax.dot_general(screen_rows, con_pairs, (((1,), (1,)), ((), ())), preferred_element_type=jnp.float32).astype(jnp.bfloat16)
    partial_sum = jnp.dot(val_pairs, interim, preferred_element_type=jnp.float32)
    partial_sum = partial_sum.reshape(val_count, val_count, con_count, con_count).transpose(0, 2, 1, 3)
    return partial_sum.reshape(val_count * con_count, val_count * con_count)


def reference(valence_bands, conduction_bands, screened, pair_list, transfer_index, owner_map):
    slot_first = jnp.take(owner_map, pair_list[:, 0]).astype(jnp.int32)
    slot_second = jnp.take(owner_map, pair_list[:, 1]).astype(jnp.int32)
    transfers = transfer_index[:, 0].astype(jnp.int32)

    def one_pair(operands):
        first_slot, second_slot, which = operands
        block = pair_kernel(valence_bands[first_slot], valence_bands[second_slot], conduction_bands[first_slot], conduction_bands[second_slot], screened[which])
        return block.astype(jnp.bfloat16)

    direct = lax.map(one_pair, (slot_first, slot_second, transfers))
    mirror_order = rank_table(slot_second, N_PB, PAIR_DEV).reshape(-1)
    mirror = jnp.transpose(jnp.take(direct, mirror_order, axis=0), (0, 2, 1))
    return direct, mirror
```

```python
import functools
import math

import jax
import jax.numpy as jnp
from jax import lax
from jax.experimental import pallas as pl
from jax.experimental.pallas import tpu as pltpu
from jax.sharding import PartitionSpec as P

PAIR_DEV = 2
MOST = 6
SUB = 8
F32, BF16, I32 = jnp.float32, jnp.bfloat16, jnp.int32
SMEM = pl.BlockSpec(memory_space=pltpu.SMEM)
VMEM = pl.BlockSpec(memory_space=pltpu.VMEM)
ANY = pl.BlockSpec(memory_space=pl.ANY)
LIVE, SWAP, FBIT, FIDX, SBIT, SIDX, ROW = range(7)


def table_body(pairs, transfers, owners, slots_out, route_out, rank, count, *, slots, groups, rows_split):
    me = lax.axis_index("pb")
    row = lax.axis_index("row")
    total = pairs.shape[0]
    partner = me ^ 1
    for q in range(groups):
        count[q] = 0
    for p in range(total):
        q = transfers[p, 0]
        rank[p] = count[q]
        count[q] = count[q] + 1
    for s in range(slots):
        for k in range(8):
            slots_out[s, k] = 0
        slots_out[s, ROW] = row

    def place(p):
        q = transfers[p, 0]
        low = q & ~1
        pos = rank[p] + jnp.where(q == low, 0, count[low])
        half = (count[low] + count[low + 1] + 1) // 2
        core = (pos >= half).astype(I32)
        return q, low | core, pos - core * half

    wanted = {}
    for d, name in ((me, 0), (partner, 1)):
        for j in range(PAIR_DEV):
            wanted[name, j] = d * PAIR_DEV + j

    def put(name, t, p):
        _, source, slot = place(p)
        away = source ^ jnp.where(name == 0, me, partner)
        route_out[name, t, 0] = away & 1
        route_out[name, t, 1] = (away >> 1) * slots + slot

    for name in range(2):
        for j in range(PAIR_DEV):
            put(name, j, wanted[name, j])
    for k in range(2):
        count[groups + k] = 0
    for p in range(total):
        q, source, slot = place(p)
        first = owners[pairs[p, 0]] ^ me
        second = owners[pairs[p, 1]] ^ me

        @pl.when(source == me)
        def _(q=q, slot=slot, first=first, second=second):
            slots_out[slot, LIVE] = 1
            slots_out[slot, SWAP] = (q != me).astype(I32)
            slots_out[slot, FBIT] = first & 1
            slots_out[slot, FIDX] = first >> 1
            slots_out[slot, SBIT] = second & 1
            slots_out[slot, SIDX] = second >> 1

        for name, d in ((0, 0), (1, 1)):
            @pl.when(second == d)
            def _(name=name, p=p):
                k = count[groups + name]
                put(name, PAIR_DEV + k, p)
                count[groups + name] = k + 1


def tables(pair_list, transfer_index, owner_map, slots, groups, rows_split):
    body = functools.partial(table_body, slots=slots, groups=groups, rows_split=rows_split)
    return pl.pallas_call(
        body,
        out_shape=[
            jax.ShapeDtypeStruct((slots, 8), I32),
            jax.ShapeDtypeStruct((2, 2 * PAIR_DEV, 2), I32),
        ],
        in_specs=[SMEM] * 3,
        out_specs=[SMEM] * 2,
        scratch_shapes=[pltpu.SMEM((pair_list.shape[0],), I32), pltpu.SMEM((groups + 2,), I32)],
    )(pair_list, transfer_index, owner_map)


def pair_body(info, own, other, w_own, w_other, *rest, slot, rows_split, parts, chunk):
    outs = rest[:rows_split]
    first_buf, second_buf, products, wbuf, interim, val_products, sem, con_sem = rest[rows_split:]
    nc, nloc = own.shape[2:]
    m = w_own.shape[0]
    nv = nc
    per = nv // rows_split
    height = val_products.shape[0] // rows_split
    step = m // parts

    @pl.when(info[slot, LIVE] != 0)
    def _():
        for bit, src in ((0, own), (1, other)):
            for which, k, buf in ((FBIT, FIDX, first_buf), (SBIT, SIDX, second_buf)):
                @pl.when(info[slot, which] == bit)
                def _(src=src, k=k, buf=buf, which=which):
                    pltpu.make_async_copy(src.at[info[slot, k]], buf, con_sem.at[which == SBIT and 1 or 0]).start()

        def w_copy(w, k):
            rows = pl.ds(k * step, step)
            return pltpu.make_async_copy(w.at[rows], wbuf.at[rows], sem.at[k])

        for which, w in ((0, w_own), (1, w_other)):
            @pl.when(info[slot, SWAP] == which)
            def _(w=w):
                for k in range(parts):
                    w_copy(w, k).start()

        pltpu.make_async_copy(own.at[0], first_buf, con_sem.at[0]).wait()
        pltpu.make_async_copy(own.at[0], second_buf, con_sem.at[1]).wait()

        def lows(n):
            rows = lax.broadcasted_iota(I32, (SUB, n), 0)
            return {i: rows < i for i in range(1, SUB)}

        def tile(lines, tiled, at, total, width, low):
            n = tiled.shape[1]
            lo, hi = min(at, total - 1) // width, min(at + SUB - 1, total - 1) // width
            left = jnp.broadcast_to(lines[lo:lo + 1], (SUB, n))
            if hi != lo:
                left = jnp.where(low[hi * width - at], left, jnp.broadcast_to(lines[hi:hi + 1], (SUB, n)))
            base = at % tiled.shape[0]
            return left * tiled[base:base + SUB]

        low = lows(chunk)
        group = 2 * SUB // math.gcd(nc, 2 * SUB)
        for j in range(rows_split):
            block = lax.rem(info[slot, ROW] - j + rows_split, rows_split)
            for k in range(0, nloc, chunk):
                lines = first_buf[j, :, k:k + chunk].astype(F32)
                tiled = jnp.concatenate([second_buf[j, :, k:k + chunk].astype(F32)] * group, axis=0)
                cols = pl.ds(pl.multiple_of(block * nloc + k, 128), chunk)
                for at in range(0, nc * nc, 2 * SUB):
                    two = [tile(lines, tiled, at + o, nc * nc, nc, low) for o in (0, SUB)]
                    products[at:at + 2 * SUB, cols] = jnp.concatenate(two, axis=0).astype(BF16)

        low = lows(nloc)
        lines = first_buf[rows_split].astype(F32)
        tiled = jnp.concatenate([second_buf[rows_split].astype(F32)] * (per + 1), axis=0)
        for s in range(rows_split):
            for at in range(0, height, SUB):
                x = tile(lines[s * per:(s + 1) * per], tiled, at, per * nv, nv, low)
                val_products[s * height + at:s * height + at + SUB, :] = x.astype(BF16)

        for k in range(parts):
            w_copy(w_own, k).wait()
            got = lax.dot_general(
                products[...], wbuf[k * step:(k + 1) * step, :], (((1,), (1,)), ((), ())), preferred_element_type=F32
            )
            interim[:, k * step:(k + 1) * step] = got.astype(BF16)
        res = lax.dot_general(
            val_products[...], interim[...], (((1,), (1,)), ((), ())), preferred_element_type=F32
        )
        for s in range(rows_split):
            for out in range(rows_split):
                @pl.when(lax.rem(info[slot, ROW] + out, rows_split) == s)
                def _(s=s, out=out):
                    outs[out][...] = res[s * height:s * height + per * nv].astype(BF16)


def pair_call(info, slot, own, other, w_own, w_other, rows_split, parts=2, chunk=256):
    nc, nloc = own.shape[2:]
    m, n = w_own.shape
    nv = nc
    per = nv // rows_split
    height = -(-per * nv // SUB) * SUB
    return pl.pallas_call(
        functools.partial(pair_body, slot=slot, rows_split=rows_split, parts=parts, chunk=chunk),
        out_shape=[jax.ShapeDtypeStruct((per * nv, nc * nc), BF16)] * rows_split,
        in_specs=[SMEM] + [ANY] * 4,
        out_specs=[VMEM] * rows_split,
        scratch_shapes=[
            pltpu.VMEM(own.shape[1:], BF16),
            pltpu.VMEM(own.shape[1:], BF16),
            pltpu.VMEM((nc * nc, n), BF16),
            pltpu.VMEM((m, n), BF16),
            pltpu.VMEM((nc * nc, m), BF16),
            pltpu.VMEM((rows_split * height, m), BF16),
            pltpu.SemaphoreType.DMA((parts,)),
            pltpu.SemaphoreType.DMA((2,)),
        ],
        compiler_params=pltpu.CompilerParams(vmem_limit_bytes=60 << 20),
        cost_estimate=pl.CostEstimate(flops=2 * nc * nc * m * n, bytes_accessed=2 * m * n, transcendentals=0),
    )(info, own, other, w_own, w_other)


def choose_body(route, *rest, held):
    blocks = rest[:held]
    mine, theirs, sem = rest[held:]
    wants = mine.shape[0]
    for name, out in ((0, mine), (1, theirs)):
        for t in range(wants):
            here = route[name, t, 0] == 0
            for i in range(held):
                @pl.when((route[name, t, 1] == i) & (here if name == 0 else ~here))
                def _(i=i, t=t, out=out, name=name):
                    pltpu.make_async_copy(blocks[i], out.at[t], sem.at[name, t]).start()
    for name, out in ((0, mine), (1, theirs)):
        for t in range(wants):
            here = route[name, t, 0] == 0
            @pl.when(here if name == 0 else ~here)
            def _(t=t, out=out, name=name):
                pltpu.make_async_copy(blocks[0], out.at[t], sem.at[name, t]).wait()


def choose(route, blocks):
    shape = (2 * PAIR_DEV,) + blocks[0].shape
    return pl.pallas_call(
        functools.partial(choose_body, held=len(blocks)),
        out_shape=[jax.ShapeDtypeStruct(shape, BF16)] * 2,
        in_specs=[SMEM] + [ANY] * len(blocks),
        out_specs=[VMEM] * 2,
        scratch_shapes=[pltpu.SemaphoreType.DMA((2, 2 * PAIR_DEV))],
    )(route, *blocks)


def shards(valence_bands, conduction_bands, screened, pair_list, transfer_index, owner_map):
    groups = lax.axis_size("pb")
    rows_split = lax.axis_size("row")
    row = lax.axis_index("row")
    total = pair_list.shape[0]
    slots = -(-min(2 * MOST, total - (groups - 2)) // 2)

    def away(x, k):
        return lax.ppermute(x, "pb", [(i, i ^ k) for i in range(groups)])

    def along(x, k):
        return lax.ppermute(x, "row", [(i, (i + k) % rows_split) for i in range(rows_split)])

    info, route = tables(pair_list, transfer_index, owner_map, slots, groups, rows_split)
    w_own = screened[0]
    w_other = away(w_own, 1)
    con = [conduction_bands] + [along(conduction_bands, s) for s in range(1, rows_split)]
    bands = jnp.concatenate(con + [valence_bands], axis=0)
    own = jnp.stack([bands] + [away(bands, 2 * k) for k in range(1, groups // 2)])
    other = away(own, 1)

    def one_slot(slot):
        pieces = pair_call(info, slot, own, other, w_own, w_other, rows_split)
        shares = [pieces[0]] + [along(pieces[s], s) for s in range(1, rows_split)]
        summed = functools.reduce(lambda a, b: a + b, [x.astype(F32) for x in shares]).astype(BF16)
        return [summed] + [away(summed, 2 * k) for k in range(1, groups // 2)]

    held = [one_slot(s) for s in range(slots)]
    blocks = [held[s][x] for x in range(groups // 2) for s in range(slots)]
    mine, theirs = choose(route, blocks)
    swapped = away(theirs, 1)
    arrived = jnp.where((route[0, :, 0] == 0)[:, None, None], mine, swapped)
    nc = conduction_bands.shape[1]
    nv = valence_bands.shape[1]
    per = nv // rows_split
    band_rows = per * nc
    direct = arrived[:PAIR_DEV].reshape(PAIR_DEV, per, nv, nc, nc).transpose(0, 1, 3, 2, 4)
    direct = direct.reshape(PAIR_DEV, band_rows, nv * nc)
    turned = arrived[PAIR_DEV:].reshape(PAIR_DEV, per, rows_split, per, nc * nc)
    got = []
    for s in range(rows_split):
        piece = lax.dynamic_index_in_dim(turned, lax.rem(row + s, rows_split), 2, keepdims=False)
        got.append(along(piece, s) if s else piece)
    places = lax.rem(row - jnp.arange(rows_split, dtype=I32) + rows_split, rows_split)
    got = jnp.stack(got)
    ordered = jnp.take(got, places, axis=0)
    mirror = ordered.reshape(rows_split, PAIR_DEV, per, per, nc, nc).transpose(1, 3, 5, 0, 2, 4)
    mirror = mirror.reshape(PAIR_DEV, band_rows, nv * nc)
    return direct, mirror


def rank_table(labels, groups, slots_per):
    total_rows = labels.shape[0]
    member = (labels[None, :] == jnp.arange(groups, dtype=jnp.int32)[:, None]).astype(jnp.int32)
    before = jnp.cumsum(member, axis=1) - 1
    placed = member[:, None, :] * (
        before[:, None, :] == jnp.arange(slots_per, dtype=jnp.int32)[None, :, None]
    ).astype(jnp.int32)
    numbers = jnp.arange(total_rows, dtype=jnp.int32) + 1
    return jnp.sum(placed * numbers[None, None, :], axis=2) - 1


def whole_pair(val_first, val_second, con_first, con_second, screen_rows):
    val_count = val_first.shape[0]
    con_count = con_first.shape[0]
    val_pairs = val_first[:, None, :].astype(jnp.float32) * val_second[None, :, :].astype(
        jnp.float32
    )
    val_pairs = val_pairs.reshape(val_count * val_count, val_first.shape[1]).astype(jnp.bfloat16)
    con_pairs = con_first[:, None, :].astype(jnp.float32) * con_second[None, :, :].astype(
        jnp.float32
    )
    con_pairs = con_pairs.reshape(con_count * con_count, con_first.shape[1]).astype(jnp.bfloat16)
    interim = lax.dot_general(
        screen_rows, con_pairs, (((1,), (1,)), ((), ())), preferred_element_type=jnp.float32
    ).astype(jnp.bfloat16)
    partial_sum = jnp.dot(val_pairs, interim, preferred_element_type=jnp.float32)
    partial_sum = partial_sum.reshape(val_count, val_count, con_count, con_count).transpose(
        0, 2, 1, 3
    )
    return partial_sum.reshape(val_count * con_count, val_count * con_count)


def plain_shards(valence_bands, conduction_bands, screened, pair_list, transfer_index, owner_map):
    groups = lax.axis_size("pb")
    rows_split = lax.axis_size("row")
    device = lax.axis_index("pb")
    val_all, con_local = (
        lax.all_gather(valence_bands, "pb", axis=0, tiled=True),
        lax.all_gather(conduction_bands, "pb", axis=0, tiled=True),
    )
    slot_table = rank_table(transfer_index[:, 0], groups, MOST)
    own_slots = lax.dynamic_index_in_dim(slot_table, device, 0, keepdims=False)
    live_pair = jnp.maximum(own_slots, 0)
    slot_first = jnp.take(owner_map, jnp.take(pair_list[:, 0], live_pair))
    slot_second = jnp.take(owner_map, jnp.take(pair_list[:, 1], live_pair))
    val_first = jnp.take(val_all, slot_first, axis=0)
    val_second = jnp.take(val_all, slot_second, axis=0)
    con_full = lax.all_gather(con_local, "row", axis=2, tiled=True)
    con_first = jnp.take(con_full, slot_first, axis=0)
    con_second = jnp.take(con_full, slot_second, axis=0)
    screen_rows = screened[0]

    def one_slot(operands):
        return whole_pair(operands[0], operands[1], operands[2], operands[3], screen_rows)

    partials = lax.map(one_slot, (val_first, val_second, con_first, con_second))
    shares = lax.psum_scatter(partials, "row", scatter_dimension=1, tiled=True).astype(jnp.bfloat16)
    band_rows = shares.shape[1]
    mirror_table = rank_table(jnp.take(owner_map, pair_list[:, 1]), groups, PAIR_DEV)
    flat_slots = slot_table.reshape(-1)
    own_direct = device * PAIR_DEV + jnp.arange(PAIR_DEV, dtype=jnp.int32)
    own_mirror = lax.dynamic_index_in_dim(mirror_table, device, 0, keepdims=False)
    wanted = jnp.concatenate([own_direct, own_mirror])
    select = (wanted[:, None] == flat_slots[None, :]).astype(jnp.bfloat16)
    arrived = jnp.einsum(
        "ji,ixy->jxy",
        select,
        lax.all_gather(shares, "pb", axis=0, tiled=True),
        preferred_element_type=jnp.float32,
    )
    direct = arrived[:PAIR_DEV].astype(jnp.bfloat16)
    mirror_rows = arrived[PAIR_DEV:].astype(jnp.bfloat16)
    turned = jnp.transpose(mirror_rows, (0, 2, 1)).reshape(
        PAIR_DEV, rows_split, band_rows, band_rows
    )
    swapped = lax.all_to_all(turned, "row", split_axis=1, concat_axis=3, tiled=True)
    mirror = swapped.reshape(PAIR_DEV, band_rows, band_rows * rows_split)
    return (direct, mirror)


def solution(mesh):
    in_specs = (P("pb", None, "row"), P("pb", None, "row"), P("pb", "row", None), P(), P(), P())
    out_specs = (P("pb", "row", None), P("pb", "row", None))

    def step(valence_bands, conduction_bands, *rest):
        groups, rows_split = mesh.shape["pb"], mesh.shape["row"]
        nv, nc = valence_bands.shape[1], conduction_bands.shape[1]
        even = nv == nc and nv % rows_split == 0 and groups & (groups - 1) == 0 and groups >= 2
        body = shards if even else plain_shards
        mapped = jax.shard_map(body, mesh=mesh, in_specs=in_specs, out_specs=out_specs, check_vma=False)
        return mapped(valence_bands, conduction_bands, *rest)

    return step
```

```python
import functools
import math

import jax
import jax.numpy as jnp
from jax import lax
from jax.experimental import pallas as pl
from jax.experimental.pallas import tpu as pltpu
from jax.sharding import PartitionSpec as P

PAIR_DEV = 2
MOST = 6
SUB = 8
F32, BF16, I32 = jnp.float32, jnp.bfloat16, jnp.int32
SMEM = pl.BlockSpec(memory_space=pltpu.SMEM)
VMEM = pl.BlockSpec(memory_space=pltpu.VMEM)
ANY = pl.BlockSpec(memory_space=pl.ANY)
LIVE, SWAP, FBIT, FIDX, SBIT, SIDX, ROW, DEEP = range(8)
GROUP = 2


def table_body(pairs, transfers, owners, slots_out, route_out, rank, count, *, slots, groups, rows_split):
    me = lax.axis_index("pb")
    row = lax.axis_index("row")
    total = pairs.shape[1]
    partner = me ^ 1
    for q in range(groups):
        count[q] = 0
    for p in range(total):
        q = transfers[p]
        rank[p] = count[q]
        count[q] = count[q] + 1
    for s in range(slots):
        for k in range(8):
            slots_out[s, k] = 0
        slots_out[s, ROW] = row
    deep = 0
    for q in range(0, groups, 2):
        deep = jnp.maximum(deep, (count[q] + count[q + 1] + 1) // 2)
    for s in range(slots):
        slots_out[s, DEEP] = deep

    def place(p):
        q = transfers[p]
        low = q & ~1
        pos = rank[p] + jnp.where(q == low, 0, count[low])
        half = (count[low] + count[low + 1] + 1) // 2
        core = (pos >= half).astype(I32)
        return q, low | core, pos - core * half

    wanted = {}
    for d, name in ((me, 0), (partner, 1)):
        for j in range(PAIR_DEV):
            wanted[name, j] = d * PAIR_DEV + j

    def put(name, t, p):
        _, source, slot = place(p)
        away = source ^ jnp.where(name == 0, me, partner)
        route_out[name, t, 0] = away & 1
        route_out[name, t, 1] = (away >> 1) * slots + slot

    for name in range(2):
        for j in range(PAIR_DEV):
            put(name, j, wanted[name, j])
    for k in range(2):
        count[groups + k] = 0
    for p in range(total):
        q, source, slot = place(p)
        first = owners[pairs[0, p]] ^ me
        second = owners[pairs[1, p]] ^ me

        @pl.when(source == me)
        def _(q=q, slot=slot, first=first, second=second):
            slots_out[slot, LIVE] = 1
            slots_out[slot, SWAP] = (q != me).astype(I32)
            slots_out[slot, FBIT] = first & 1
            slots_out[slot, FIDX] = first >> 1
            slots_out[slot, SBIT] = second & 1
            slots_out[slot, SIDX] = second >> 1

        for name, d in ((0, 0), (1, 1)):
            @pl.when(second == d)
            def _(name=name, p=p):
                k = count[groups + name]
                put(name, PAIR_DEV + k, p)
                count[groups + name] = k + 1


def tables(pair_list, transfer_index, owner_map, slots, groups, rows_split):
    body = functools.partial(table_body, slots=slots, groups=groups, rows_split=rows_split)
    return pl.pallas_call(
        body,
        out_shape=[
            jax.ShapeDtypeStruct((slots, 8), I32),
            jax.ShapeDtypeStruct((2, 2 * PAIR_DEV, 2), I32),
        ],
        in_specs=[SMEM] * 3,
        out_specs=[SMEM] * 2,
        scratch_shapes=[pltpu.SMEM((pair_list.shape[0],), I32), pltpu.SMEM((groups + 2,), I32)],
    )(pair_list.T, transfer_index.reshape(-1), owner_map)


def pair_body(info, own, own_rest, other, other_rest, w_own, w_other, *rest, slots, rows_split, parts, chunk):
    outs = rest[:rows_split]
    near, far, products, wbuf, interim, val_products, result, sem, con_sem = rest[rows_split:]
    nc = own.shape[1] // 2
    nloc = own.shape[2]
    m = w_own.shape[0]
    nv = nc
    per = nv // rows_split
    height = val_products.shape[0] // rows_split
    step = m // parts
    base = slots[0]
    row = info[base, ROW]

    def band_copies(i, which, bit):
        k = info[base + i, FIDX if which == 0 else SIDX]
        src, src_rest = (own, own_rest) if bit == 0 else (other, other_rest)
        return (
            pltpu.make_async_copy(src.at[k], near.at[i, which], con_sem.at[0, i, which]),
            pltpu.make_async_copy(src_rest.at[k], far.at[i, which], con_sem.at[1, i, which]),
        )

    def w_copy(which, k):
        rows = pl.ds(k * step, step)
        return pltpu.make_async_copy((w_own, w_other)[which].at[rows], wbuf.at[which, rows], sem.at[which, k])

    count = len(slots)
    live = [info[s, LIVE] != 0 for s in slots]
    for i in range(count):
        for which, flag in ((0, FBIT), (1, SBIT)):
            for bit in range(2):
                @pl.when(live[i] & (info[slots[i], flag] == bit))
                def _(i=i, which=which, bit=bit):
                    for c in band_copies(i, which, bit):
                        c.start()
        for which in range(2):
            new = live[i] & (info[slots[i], SWAP] == which)
            for before in range(i):
                new = new & ~(live[before] & (info[slots[before], SWAP] == which))
            @pl.when(new)
            def _(which=which):
                for k in range(parts):
                    w_copy(which, k).start()

    def lows(n):
        rows = lax.broadcasted_iota(I32, (SUB, n), 0)
        return {i: rows < i for i in range(1, SUB)}

    def tile(lines, tiled, at, total, width, low):
        n = tiled.shape[1]
        lo, hi = min(at, total - 1) // width, min(at + SUB - 1, total - 1) // width
        left = jnp.broadcast_to(lines[lo:lo + 1], (SUB, n))
        if hi != lo:
            left = jnp.where(low[hi * width - at], left, jnp.broadcast_to(lines[hi:hi + 1], (SUB, n)))
        start = at % tiled.shape[0]
        return left * tiled[start:start + SUB]

    group = 2 * SUB // math.gcd(nc, 2 * SUB)

    @pl.loop(0, count)
    def _(i):
        slot = base + i

        @pl.when(info[slot, LIVE] != 0)
        def _():
            for which in range(2):
                pltpu.make_async_copy(own.at[0], near.at[i, which], con_sem.at[0, i, which]).wait()
                pltpu.make_async_copy(own_rest.at[0], far.at[i, which], con_sem.at[1, i, which]).wait()
            low = lows(chunk)
            for j in range(rows_split):
                block = lax.rem(row - j + rows_split, rows_split)
                for k in range(0, nloc, chunk):
                    def band(which):
                        if j == 0:
                            return near[i, which, :, k:k + chunk].astype(F32)[:nc]
                        return far[i, which, :, k:k + chunk].astype(F32)[(j - 1) * nc:j * nc]
                    lines = band(0)
                    tiled = jnp.concatenate([band(1)] * group, axis=0)
                    cols = pl.ds(pl.multiple_of(block * nloc + k, 128), chunk)
                    for at in range(0, nc * nc, 2 * SUB):
                        two = [tile(lines, tiled, at + o, nc * nc, nc, low) for o in (0, SUB)]
                        products[at:at + 2 * SUB, cols] = jnp.concatenate(two, axis=0).astype(BF16)

            low = lows(nloc)
            lines = near[i, 0].astype(F32)[nc:]
            tiled = jnp.concatenate([near[i, 1].astype(F32)[nc:]] * (per + 1), axis=0)
            for s in range(rows_split):
                for at in range(0, height, SUB):
                    x = tile(lines[s * per:(s + 1) * per], tiled, at, per * nv, nv, low)
                    val_products[s * height + at:s * height + at + SUB, :] = x.astype(BF16)

            swap = info[slot, SWAP]
            fresh = jnp.bool_(True)
            for before in range(count):
                used = live[before] & (info[slots[before], SWAP] == swap) & (before < i)
                fresh = fresh & ~used
            for k in range(parts):
                for which in range(2):
                    @pl.when(fresh & (swap == which))
                    def _(which=which, k=k):
                        w_copy(which, k).wait()
                got = lax.dot_general(
                    products[...], wbuf[swap, k * step:(k + 1) * step, :], (((1,), (1,)), ((), ())),
                    preferred_element_type=F32,
                )
                interim[:, k * step:(k + 1) * step] = got.astype(BF16)
            res = lax.dot_general(
                val_products[...], interim[...], (((1,), (1,)), ((), ())), preferred_element_type=F32
            )
            for s in range(rows_split):
                result[s] = res[s * height:(s + 1) * height]
            for g in range(count):
                @pl.when(i == g)
                def _(g=g):
                    for s in range(rows_split):
                        piece = result[lax.rem(row + s, rows_split)]
                        outs[s][:, g * nc * nc:(g + 1) * nc * nc] = piece[:per * nv].astype(BF16)


def pair_call(info, slots, own, own_rest, other, other_rest, w_own, w_other, rows_split, parts=2, chunk=256):
    nc, nloc = own.shape[1] // 2, own.shape[2]
    m, n = w_own.shape
    nv = nc
    per = nv // rows_split
    height = -(-per * nv // SUB) * SUB
    count = len(slots)
    return pl.pallas_call(
        functools.partial(pair_body, slots=slots, rows_split=rows_split, parts=parts, chunk=chunk),
        out_shape=[jax.ShapeDtypeStruct((per * nv, count * nc * nc), BF16)] * rows_split,
        in_specs=[SMEM] + [ANY] * 6,
        out_specs=[VMEM] * rows_split,
        scratch_shapes=[
            pltpu.VMEM((count, 2) + own.shape[1:], BF16),
            pltpu.VMEM((count, 2) + own_rest.shape[1:], BF16),
            pltpu.VMEM((nc * nc, n), BF16),
            pltpu.VMEM((2, m, n), BF16),
            pltpu.VMEM((nc * nc, m), BF16),
            pltpu.VMEM((rows_split * height, m), BF16),
            pltpu.VMEM((rows_split, height, nc * nc), F32),
            pltpu.SemaphoreType.DMA((2, parts)),
            pltpu.SemaphoreType.DMA((2, count, 2)),
        ],
        compiler_params=pltpu.CompilerParams(vmem_limit_bytes=60 << 20),
        cost_estimate=pl.CostEstimate(
            flops=2 * count * nc * nc * m * n, bytes_accessed=2 * m * n, transcendentals=0
        ),
    )(info, own, own_rest, other, other_rest, w_own, w_other)


def choose_body(route, *rest, held, slots, places):
    blocks = rest[:held]
    mine, theirs, sem = rest[held:]
    wants = mine.shape[0]
    for name, out in ((0, mine), (1, theirs)):
        for t in range(wants):
            here = (route[name, t, 0] == 0) if name == 0 else (route[name, t, 0] != 0)
            for i in range(held * GROUP):
                x, slot = i // ((held // places) * GROUP), i % ((held // places) * GROUP)
                if slot >= slots:
                    continue
                @pl.when((route[name, t, 1] == x * slots + slot) & here)
                def _(x=x, slot=slot, t=t, out=out, name=name):
                    src = blocks[x * ((held // places)) + slot // GROUP]
                    pltpu.make_async_copy(src.at[slot % GROUP], out.at[t], sem.at[name, t]).start()
    for name, out in ((0, mine), (1, theirs)):
        for t in range(wants):
            here = (route[name, t, 0] == 0) if name == 0 else (route[name, t, 0] != 0)
            @pl.when(here)
            def _(t=t, out=out, name=name):
                pltpu.make_async_copy(blocks[0].at[0], out.at[t], sem.at[name, t]).wait()


def choose(route, blocks, slots, places):
    shape = (2 * PAIR_DEV,) + blocks[0].shape[1:]
    return pl.pallas_call(
        functools.partial(choose_body, held=len(blocks), slots=slots, places=places),
        out_shape=[jax.ShapeDtypeStruct(shape, BF16)] * 2,
        in_specs=[SMEM] + [ANY] * len(blocks),
        out_specs=[VMEM] * 2,
        scratch_shapes=[pltpu.SemaphoreType.DMA((2, 2 * PAIR_DEV))],
    )(route, *blocks)


def split_body(route, info, mine, swapped, direct, *rest, rows_split):
    outs, turned = rest[:rows_split], rest[rows_split]
    row = info[0, ROW]
    width = direct.shape[2] // rows_split
    for t in range(2 * PAIR_DEV):
        x = jnp.where(route[0, t, 0] == 0, mine[t].astype(F32), swapped[t].astype(F32))
        if t < PAIR_DEV:
            direct[t] = x.astype(BF16)
        else:
            x = x.T
            for s in range(rows_split):
                turned[t - PAIR_DEV, s] = x[s * width:(s + 1) * width]
    for s in range(rows_split):
        for t in range(PAIR_DEV):
            outs[s][t] = turned[t, lax.rem(row + s, rows_split)].astype(BF16)


def split(route, info, mine, swapped, rows_split):
    rows, columns = mine.shape[1:]
    width = columns // rows_split
    return pl.pallas_call(
        functools.partial(split_body, rows_split=rows_split),
        out_shape=[jax.ShapeDtypeStruct((PAIR_DEV, rows, columns), BF16)]
        + [jax.ShapeDtypeStruct((PAIR_DEV, width, rows), BF16)] * rows_split,
        in_specs=[SMEM, SMEM, VMEM, VMEM],
        out_specs=[VMEM] * (rows_split + 1),
        scratch_shapes=[pltpu.VMEM((PAIR_DEV, rows_split, width, rows), F32)],
    )(route, info, mine, swapped)


def join_body(info, *rest, rows_split):
    pieces, mirror, placed = rest[:rows_split], rest[rows_split], rest[rows_split + 1]
    row = info[0, ROW]
    width = pieces[0].shape[2]
    for s in range(rows_split):
        for t in range(PAIR_DEV):
            placed[t, lax.rem(row - s + rows_split, rows_split)] = pieces[s][t].astype(F32)
    for t in range(PAIR_DEV):
        mirror[t] = jnp.concatenate([placed[t, s] for s in range(rows_split)], axis=1).astype(BF16)


def join(info, pieces):
    rows_split = len(pieces)
    _, height, width = pieces[0].shape
    return pl.pallas_call(
        functools.partial(join_body, rows_split=rows_split),
        out_shape=jax.ShapeDtypeStruct((PAIR_DEV, height, width * rows_split), BF16),
        in_specs=[SMEM] + [VMEM] * rows_split,
        out_specs=VMEM,
        scratch_shapes=[pltpu.VMEM((PAIR_DEV, rows_split, height, width), F32)],
    )(info, *pieces)


def shards(valence_bands, conduction_bands, screened, pair_list, transfer_index, owner_map):
    groups = lax.axis_size("pb")
    rows_split = lax.axis_size("row")
    total = pair_list.shape[0]
    slots = -(-min(2 * MOST, total - (groups - 2)) // 2)
    nc, nv = conduction_bands.shape[1], valence_bands.shape[1]
    per = nv // rows_split

    def away(x, k):
        return lax.ppermute(x, "pb", [(i, i ^ k) for i in range(groups)])

    def along(x, k):
        return lax.ppermute(x, "row", [(i, (i + k) % rows_split) for i in range(rows_split)])

    w_own = screened[0]
    w_other = away(w_own, 1)
    bands = jnp.concatenate([conduction_bands[0], valence_bands[0]], axis=0)
    con = [along(conduction_bands[0], s) for s in range(1, rows_split)]
    info, route = tables(pair_list, transfer_index, owner_map, slots, groups, rows_split)
    own = jnp.stack([bands] + [away(bands, 2 * k) for k in range(1, groups // 2)])
    con_rest = jnp.concatenate(con, axis=0)
    con_rest, info, route = lax.optimization_barrier((con_rest, info, route))
    own_rest = jnp.stack([con_rest] + [away(con_rest, 2 * k) for k in range(1, groups // 2)])
    other = away(own, 1)
    other_rest = away(own_rest, 1)

    def some_slots(which):
        pieces = pair_call(info, which, own, own_rest, other, other_rest, w_own, w_other, rows_split)
        shares = [pieces[0]] + [along(pieces[s], s) for s in range(1, rows_split)]
        return functools.reduce(lambda a, b: a + b, [x.astype(F32) for x in shares]).astype(BF16)

    def spread(summed, count):
        x = summed.reshape(per, nv, count, nc, nc).transpose(2, 0, 3, 1, 4).reshape(count, per * nc, nv * nc)
        return [x] + [away(x, 2 * k) for k in range(1, groups // 2)]

    def finish(held):
        blocks = [h[x] for x in range(groups // 2) for h in held]
        mine, theirs = choose(route, blocks, slots, groups // 2)
        swapped = away(theirs, 1)
        direct, *pieces = split(route, info, mine, swapped, rows_split)
        got = [pieces[0]] + [along(pieces[s], s) for s in range(1, rows_split)]
        return direct, join(info, got)

    usual = min(slots, 2 * GROUP)
    held = []
    for s in range(0, usual, GROUP):
        which = tuple(range(s, min(s + GROUP, slots)))
        held.append(spread(some_slots(which), len(which)))
    if slots <= usual:
        return finish(held)

    def deep():
        more = []
        for s in range(usual, slots, GROUP):
            which = tuple(range(s, min(s + GROUP, slots)))
            more.append(spread(some_slots(which), len(which)))
        return finish(held + more)

    return lax.cond(info[0, DEEP] > usual, deep, lambda: finish(held))


def rank_table(labels, groups, slots_per):
    total_rows = labels.shape[0]
    member = (labels[None, :] == jnp.arange(groups, dtype=jnp.int32)[:, None]).astype(jnp.int32)
    before = jnp.cumsum(member, axis=1) - 1
    placed = member[:, None, :] * (
        before[:, None, :] == jnp.arange(slots_per, dtype=jnp.int32)[None, :, None]
    ).astype(jnp.int32)
    numbers = jnp.arange(total_rows, dtype=jnp.int32) + 1
    return jnp.sum(placed * numbers[None, None, :], axis=2) - 1


def whole_pair(val_first, val_second, con_first, con_second, screen_rows):
    val_count = val_first.shape[0]
    con_count = con_first.shape[0]
    val_pairs = val_first[:, None, :].astype(jnp.float32) * val_second[None, :, :].astype(
        jnp.float32
    )
    val_pairs = val_pairs.reshape(val_count * val_count, val_first.shape[1]).astype(jnp.bfloat16)
    con_pairs = con_first[:, None, :].astype(jnp.float32) * con_second[None, :, :].astype(
        jnp.float32
    )
    con_pairs = con_pairs.reshape(con_count * con_count, con_first.shape[1]).astype(jnp.bfloat16)
    interim = lax.dot_general(
        screen_rows, con_pairs, (((1,), (1,)), ((), ())), preferred_element_type=jnp.float32
    ).astype(jnp.bfloat16)
    partial_sum = jnp.dot(val_pairs, interim, preferred_element_type=jnp.float32)
    partial_sum = partial_sum.reshape(val_count, val_count, con_count, con_count).transpose(
        0, 2, 1, 3
    )
    return partial_sum.reshape(val_count * con_count, val_count * con_count)


def plain_shards(valence_bands, conduction_bands, screened, pair_list, transfer_index, owner_map):
    groups = lax.axis_size("pb")
    rows_split = lax.axis_size("row")
    device = lax.axis_index("pb")
    val_all, con_local = (
        lax.all_gather(valence_bands, "pb", axis=0, tiled=True),
        lax.all_gather(conduction_bands, "pb", axis=0, tiled=True),
    )
    slot_table = rank_table(transfer_index[:, 0], groups, MOST)
    own_slots = lax.dynamic_index_in_dim(slot_table, device, 0, keepdims=False)
    live_pair = jnp.maximum(own_slots, 0)
    slot_first = jnp.take(owner_map, jnp.take(pair_list[:, 0], live_pair))
    slot_second = jnp.take(owner_map, jnp.take(pair_list[:, 1], live_pair))
    val_first = jnp.take(val_all, slot_first, axis=0)
    val_second = jnp.take(val_all, slot_second, axis=0)
    con_full = lax.all_gather(con_local, "row", axis=2, tiled=True)
    con_first = jnp.take(con_full, slot_first, axis=0)
    con_second = jnp.take(con_full, slot_second, axis=0)
    screen_rows = screened[0]

    def one_slot(operands):
        return whole_pair(operands[0], operands[1], operands[2], operands[3], screen_rows)

    partials = lax.map(one_slot, (val_first, val_second, con_first, con_second))
    shares = lax.psum_scatter(partials, "row", scatter_dimension=1, tiled=True).astype(jnp.bfloat16)
    band_rows = shares.shape[1]
    mirror_table = rank_table(jnp.take(owner_map, pair_list[:, 1]), groups, PAIR_DEV)
    flat_slots = slot_table.reshape(-1)
    own_direct = device * PAIR_DEV + jnp.arange(PAIR_DEV, dtype=jnp.int32)
    own_mirror = lax.dynamic_index_in_dim(mirror_table, device, 0, keepdims=False)
    wanted = jnp.concatenate([own_direct, own_mirror])
    select = (wanted[:, None] == flat_slots[None, :]).astype(jnp.bfloat16)
    arrived = jnp.einsum(
        "ji,ixy->jxy",
        select,
        lax.all_gather(shares, "pb", axis=0, tiled=True),
        preferred_element_type=jnp.float32,
    )
    direct = arrived[:PAIR_DEV].astype(jnp.bfloat16)
    mirror_rows = arrived[PAIR_DEV:].astype(jnp.bfloat16)
    turned = jnp.transpose(mirror_rows, (0, 2, 1)).reshape(
        PAIR_DEV, rows_split, band_rows, band_rows
    )
    swapped = lax.all_to_all(turned, "row", split_axis=1, concat_axis=3, tiled=True)
    mirror = swapped.reshape(PAIR_DEV, band_rows, band_rows * rows_split)
    return (direct, mirror)


def solution(mesh):
    in_specs = (P("pb", None, "row"), P("pb", None, "row"), P("pb", "row", None), P(), P(), P())
    out_specs = (P("pb", "row", None), P("pb", "row", None))

    def step(valence_bands, conduction_bands, *rest):
        groups, rows_split = mesh.shape["pb"], mesh.shape["row"]
        nv, nc = valence_bands.shape[1], conduction_bands.shape[1]
        even = nv == nc and nv % rows_split == 0 and groups & (groups - 1) == 0 and groups >= 4
        body = shards if even else plain_shards
        mapped = jax.shard_map(body, mesh=mesh, in_specs=in_specs, out_specs=out_specs, check_vma=False)
        return mapped(valence_bands, conduction_bands, *rest)

    return step
```

```python
import functools
import math

import jax
import jax.numpy as jnp
from jax import lax
from jax.experimental import pallas as pl
from jax.experimental.pallas import tpu as pltpu
from jax.sharding import PartitionSpec as P


PAIR_DEV = 2
MOST = 6
SUB = 8
F32, BF16, I32 = jnp.float32, jnp.bfloat16, jnp.int32
SMEM = pl.BlockSpec(memory_space=pltpu.SMEM)
VMEM = pl.BlockSpec(memory_space=pltpu.VMEM)
ANY = pl.BlockSpec(memory_space=pl.ANY)
LIVE, SWAP, FBIT, FIDX, SBIT, SIDX, ROW, DEEP = range(8)
GROUP = 2


def table_body(pairs, transfers, owners, slots_out, route_out, rank, count, *, slots, groups, rows_split):
    me = lax.axis_index("pb")
    row = lax.axis_index("row")
    total = pairs.shape[1]
    partner = me ^ 1
    for q in range(groups):
        count[q] = 0
    for p in range(total):
        q = transfers[p]
        rank[p] = count[q]
        count[q] = count[q] + 1
    for s in range(slots):
        for k in range(8):
            slots_out[s, k] = 0
        slots_out[s, ROW] = row
    deep = 0
    for q in range(0, groups, 2):
        deep = jnp.maximum(deep, (count[q] + count[q + 1] + 1) // 2)
    for s in range(slots):
        slots_out[s, DEEP] = deep

    def place(p):
        q = transfers[p]
        low = q & ~1
        pos = rank[p] + jnp.where(q == low, 0, count[low])
        half = (count[low] + count[low + 1] + 1) // 2
        core = (pos >= half).astype(I32)
        return q, low | core, pos - core * half

    wanted = {}
    for d, name in ((me, 0), (partner, 1)):
        for j in range(PAIR_DEV):
            wanted[name, j] = d * PAIR_DEV + j

    def put(name, t, p):
        _, source, slot = place(p)
        away = source ^ jnp.where(name == 0, me, partner)
        route_out[name, t, 0] = away & 1
        route_out[name, t, 1] = (away >> 1) * (-(-slots // GROUP) * GROUP) + slot

    for name in range(2):
        for j in range(PAIR_DEV):
            put(name, j, wanted[name, j])
    for k in range(2):
        count[groups + k] = 0
    for p in range(total):
        q, source, slot = place(p)
        first = owners[pairs[0, p]] ^ me
        second = owners[pairs[1, p]] ^ me

        @pl.when(source == me)
        def _(q=q, slot=slot, first=first, second=second):
            slots_out[slot, LIVE] = 1
            slots_out[slot, SWAP] = (q != me).astype(I32)
            slots_out[slot, FBIT] = first & 1
            slots_out[slot, FIDX] = first >> 1
            slots_out[slot, SBIT] = second & 1
            slots_out[slot, SIDX] = second >> 1

        for name, d in ((0, 0), (1, 1)):
            @pl.when(second == d)
            def _(name=name, p=p):
                k = count[groups + name]
                put(name, PAIR_DEV + k, p)
                count[groups + name] = k + 1


def tables(pair_list, transfer_index, owner_map, slots, groups, rows_split):
    body = functools.partial(table_body, slots=slots, groups=groups, rows_split=rows_split)
    return pl.pallas_call(
        body,
        out_shape=[
            jax.ShapeDtypeStruct((slots, 8), I32),
            jax.ShapeDtypeStruct((2, 2 * PAIR_DEV, 2), I32),
        ],
        in_specs=[SMEM] * 3,
        out_specs=[SMEM] * 2,
        scratch_shapes=[pltpu.SMEM((pair_list.shape[0],), I32), pltpu.SMEM((groups + 2,), I32)],
    )(pair_list.T, transfer_index.reshape(-1), owner_map)


def pair_body(info, own, own_rest, other, other_rest, w_own, w_other, *rest, slots, rows_split, parts, chunk):
    outs = rest[:rows_split]
    near, far, products, wbuf, interim, val_products, result, sem, con_sem = rest[rows_split:]
    nc = own.shape[1] // 2
    nloc = own.shape[2]
    m = w_own.shape[0]
    nv = nc
    per = nv // rows_split
    height = val_products.shape[0] // rows_split
    step = m // parts
    base = slots[0]
    row = info[base, ROW]

    def band_copies(i, which, bit):
        k = info[base + i, FIDX if which == 0 else SIDX]
        src, src_rest = (own, own_rest) if bit == 0 else (other, other_rest)
        return (
            pltpu.make_async_copy(src.at[k], near.at[i, which], con_sem.at[0, i, which]),
            pltpu.make_async_copy(src_rest.at[k], far.at[i, which], con_sem.at[1, i, which]),
        )

    def w_copy(which, k):
        rows = pl.ds(k * step, step)
        return pltpu.make_async_copy((w_own, w_other)[which].at[rows], wbuf.at[which, rows], sem.at[which, k])

    count = len(slots)
    live = [info[s, LIVE] != 0 for s in slots]
    for i in range(count):
        for which, flag in ((0, FBIT), (1, SBIT)):
            for bit in range(2):
                @pl.when(live[i] & (info[slots[i], flag] == bit))
                def _(i=i, which=which, bit=bit):
                    for c in band_copies(i, which, bit):
                        c.start()
        for which in range(2):
            new = live[i] & (info[slots[i], SWAP] == which)
            for before in range(i):
                new = new & ~(live[before] & (info[slots[before], SWAP] == which))

            @pl.when(new)
            def _(which=which):
                for k in range(parts):
                    w_copy(which, k).start()

    def lows(n):
        rows = lax.broadcasted_iota(I32, (SUB, n), 0)
        return {i: rows < i for i in range(1, SUB)}

    def tile(lines, tiled, at, total, width, low):
        n = tiled.shape[1]
        lo, hi = min(at, total - 1) // width, min(at + SUB - 1, total - 1) // width
        left = jnp.broadcast_to(lines[lo:lo + 1], (SUB, n))
        if hi != lo:
            left = jnp.where(low[hi * width - at], left, jnp.broadcast_to(lines[hi:hi + 1], (SUB, n)))
        start = at % tiled.shape[0]
        return left * tiled[start:start + SUB]

    group = 2 * SUB // math.gcd(nc, 2 * SUB)

    @pl.loop(0, count)
    def _(i):
        slot = base + i

        @pl.when(info[slot, LIVE] != 0)
        def _():
            for which in range(2):
                pltpu.make_async_copy(own.at[0], near.at[i, which], con_sem.at[0, i, which]).wait()
                pltpu.make_async_copy(own_rest.at[0], far.at[i, which], con_sem.at[1, i, which]).wait()
            low = lows(chunk)
            for j in range(rows_split):
                block = row ^ j
                for k in range(0, nloc, chunk):
                    def band(which):
                        if j == 0:
                            return near[i, which, :, k:k + chunk].astype(F32)[:nc]
                        return far[i, which, :, k:k + chunk].astype(F32)[(j - 1) * nc:j * nc]

                    lines = band(0)
                    tiled = jnp.concatenate([band(1)] * group, axis=0)
                    cols = pl.ds(pl.multiple_of(block * nloc + k, 128), chunk)
                    for at in range(0, nc * nc, 2 * SUB):
                        two = [tile(lines, tiled, at + o, nc * nc, nc, low) for o in (0, SUB)]
                        products[at:at + 2 * SUB, cols] = jnp.concatenate(two, axis=0).astype(BF16)

            low = lows(nloc)
            lines = near[i, 0].astype(F32)[nc:]
            tiled = jnp.concatenate([near[i, 1].astype(F32)[nc:]] * (per + 1), axis=0)
            for s in range(rows_split):
                for at in range(0, height, SUB):
                    x = tile(lines[s * per:(s + 1) * per], tiled, at, per * nv, nv, low)
                    val_products[s * height + at:s * height + at + SUB, :] = x.astype(BF16)

            swap = info[slot, SWAP]
            fresh = jnp.bool_(True)
            for before in range(count):
                used = live[before] & (info[slots[before], SWAP] == swap) & (before < i)
                fresh = fresh & ~used
            for k in range(parts):
                for which in range(2):
                    @pl.when(fresh & (swap == which))
                    def _(which=which, k=k):
                        w_copy(which, k).wait()
                got = lax.dot_general(
                    products[...], wbuf[swap, k * step:(k + 1) * step, :], (((1,), (1,)), ((), ())),
                    preferred_element_type=F32,
                )
                interim[:, k * step:(k + 1) * step] = got.astype(BF16)
            res = lax.dot_general(
                val_products[...], interim[...], (((1,), (1,)), ((), ())), preferred_element_type=F32
            )
            for s in range(rows_split):
                result[s] = res[s * height:(s + 1) * height]
            for g in range(count):
                @pl.when(i == g)
                def _(g=g):
                    for s in range(rows_split):
                        piece = result[row ^ s]
                        outs[s][:, g * nc * nc:(g + 1) * nc * nc] = piece[:per * nv].astype(BF16)


def pair_call(info, slots, own, own_rest, other, other_rest, w_own, w_other, rows_split, parts=2, chunk=256):
    nc = own.shape[1] // 2
    m, n = w_own.shape
    nv = nc
    per = nv // rows_split
    height = -(-per * nv // SUB) * SUB
    count = len(slots)
    return pl.pallas_call(
        functools.partial(pair_body, slots=slots, rows_split=rows_split, parts=parts, chunk=chunk),
        out_shape=[jax.ShapeDtypeStruct((per * nv, count * nc * nc), BF16)] * rows_split,
        in_specs=[SMEM] + [ANY] * 6,
        out_specs=[VMEM] * rows_split,
        scratch_shapes=[
            pltpu.VMEM((count, 2) + own.shape[1:], BF16),
            pltpu.VMEM((count, 2) + own_rest.shape[1:], BF16),
            pltpu.VMEM((nc * nc, n), BF16),
            pltpu.VMEM((2, m, n), BF16),
            pltpu.VMEM((nc * nc, m), BF16),
            pltpu.VMEM((rows_split * height, m), BF16),
            pltpu.VMEM((rows_split, height, nc * nc), F32),
            pltpu.SemaphoreType.DMA((2, parts)),
            pltpu.SemaphoreType.DMA((2, count, 2)),
        ],
        compiler_params=pltpu.CompilerParams(vmem_limit_bytes=60 << 20),
        cost_estimate=pl.CostEstimate(
            flops=2 * count * nc * nc * m * n, bytes_accessed=2 * m * n, transcendentals=0
        ),
    )(info, own, own_rest, other, other_rest, w_own, w_other)


def fetch(route, near, far, held, sem, wants):
    for i, t in enumerate(wants):
        code = route[0, t, 1]
        for bit, blocks in ((0, near), (1, far)):
            @pl.when(route[0, t, 0] == bit)
            def _(i=i, code=code, blocks=blocks):
                for k, block in enumerate(blocks):
                    @pl.when(code // GROUP == k)
                    def _(block=block):
                        pltpu.make_async_copy(block.at[code % GROUP], held.at[i], sem.at[i]).start()
    for i in range(len(wants)):
        pltpu.make_async_copy(near[0].at[0], held.at[i], sem.at[i]).wait()


def direct_body(route, *rest):
    blocks, direct, sem = rest[:-2], rest[-2], rest[-1]
    half = len(blocks) // 2
    fetch(route, blocks[:half], blocks[half:], direct, sem, range(PAIR_DEV))


def direct_rows(route, near, far):
    return pl.pallas_call(
        direct_body,
        out_shape=jax.ShapeDtypeStruct((PAIR_DEV,) + near[0].shape[1:], BF16),
        in_specs=[SMEM] + [ANY] * (2 * len(near)),
        out_specs=VMEM,
        scratch_shapes=[pltpu.SemaphoreType.DMA((PAIR_DEV,))],
    )(route, *near, *far)


def turn_body(route, info, *rest, rows_split):
    blocks, outs = rest[:-(rows_split + 3)], rest[-(rows_split + 3):-3]
    held, turned, sem = rest[-3:]
    half = len(blocks) // 2
    fetch(route, blocks[:half], blocks[half:], held, sem, range(PAIR_DEV, 2 * PAIR_DEV))
    row = info[0, ROW]
    width = turned.shape[2]
    for t in range(PAIR_DEV):
        x = held[t].astype(F32).T
        for s in range(rows_split):
            turned[t, s] = x[s * width:(s + 1) * width]
    for s in range(rows_split):
        for t in range(PAIR_DEV):
            outs[s][t] = turned[t, row ^ s].astype(BF16)


def turn(route, info, near, far, rows_split):
    rows, columns = near[0].shape[1:]
    width = columns // rows_split
    return pl.pallas_call(
        functools.partial(turn_body, rows_split=rows_split),
        out_shape=[jax.ShapeDtypeStruct((PAIR_DEV, width, rows), BF16)] * rows_split,
        in_specs=[SMEM, SMEM] + [ANY] * (2 * len(near)),
        out_specs=[VMEM] * rows_split,
        scratch_shapes=[
            pltpu.VMEM((PAIR_DEV, rows, columns), BF16),
            pltpu.VMEM((PAIR_DEV, rows_split, width, rows), F32),
            pltpu.SemaphoreType.DMA((PAIR_DEV,)),
        ],
    )(route, info, *near, *far)


def join_body(info, *rest, rows_split):
    pieces, mirror, placed = rest[:rows_split], rest[rows_split], rest[rows_split + 1]
    row = info[0, ROW]
    for s in range(rows_split):
        for t in range(PAIR_DEV):
            placed[t, row ^ s] = pieces[s][t].astype(F32)
    whole = [jnp.concatenate([placed[t, s] for s in range(rows_split)], axis=1) for t in range(PAIR_DEV)]
    mirror[...] = jnp.stack(whole, axis=1).astype(BF16)


def join(info, pieces):
    rows_split = len(pieces)
    _, height, width = pieces[0].shape
    return pl.pallas_call(
        functools.partial(join_body, rows_split=rows_split),
        out_shape=jax.ShapeDtypeStruct((height, PAIR_DEV, width * rows_split), BF16),
        in_specs=[SMEM] + [VMEM] * rows_split,
        out_specs=VMEM,
        scratch_shapes=[pltpu.VMEM((PAIR_DEV, rows_split, height, width), F32)],
    )(info, *pieces)


def shards(valence_bands, conduction_bands, screened, pair_list, transfer_index, owner_map):
    groups = lax.axis_size("pb")
    rows_split = lax.axis_size("row")
    total = pair_list.shape[0]
    slots = -(-min(2 * MOST, total - (groups - 2)) // 2)
    nc, nv = conduction_bands.shape[1], valence_bands.shape[1]
    per = nv // rows_split

    def away(x, k):
        return lax.ppermute(x, "pb", [(i, i ^ k) for i in range(groups)])

    def along(x, k):
        return lax.ppermute(x, "row", [(i, i ^ k) for i in range(rows_split)])

    w_own = screened[0]
    w_other = away(w_own, 1)
    bands = jnp.concatenate([conduction_bands[0], valence_bands[0]], axis=0)
    con = []
    for s in range(1, rows_split):
        con.append(along(conduction_bands[0], s))
    info, route = tables(pair_list, transfer_index, owner_map, slots, groups, rows_split)
    own = jnp.stack([bands] + [away(bands, 2 * k) for k in range(1, groups // 2)])
    con_rest = jnp.concatenate(con, axis=0)
    con_rest, info, route = lax.optimization_barrier((con_rest, info, route))
    own_rest = jnp.stack([con_rest] + [away(con_rest, 2 * k) for k in range(1, groups // 2)])
    other = away(own, 1)
    other_rest = away(own_rest, 1)

    before = []

    def some_slots(which, early=None):
        table = info
        if before:
            table, _ = lax.optimization_barrier((info, before[-1]))
        pieces = pair_call(table, which, own, own_rest, other, other_rest, w_own, w_other, rows_split)
        before.append(pieces[0])
        shares = [pieces[0]]
        for s in range(1, rows_split):
            shares.append(along(pieces[s], s))
        if early is not None:
            shares, early[:] = lax.optimization_barrier((shares, list(early)))
        return functools.reduce(lambda a, b: a + b, [x.astype(F32) for x in shares]).astype(BF16)

    def spread(summed, count):
        x = summed.reshape(per, nv, count, nc, nc).transpose(2, 0, 3, 1, 4).reshape(count, per * nc, nv * nc)
        out = [x]
        for k in range(1, groups // 2):
            out.append(away(x, 2 * k))
        return out + [away(x, 1) for x in out]

    def group_of(s, early=None):
        which = tuple(range(s, min(s + GROUP, slots)))
        return spread(some_slots(which, early), len(which))

    usual = min(slots, 2 * GROUP)
    more = []
    if slots > usual:
        shape = (per * nc, nv * nc)

        def deep():
            before.clear()
            more = [group_of(s) for s in range(usual, slots, GROUP)]
            return [x for m in more for x in m]

        def flat():
            counts = [min(GROUP, slots - s) for s in range(usual, slots, GROUP)]
            return [jnp.zeros((count,) + shape, BF16) for count in counts for _ in range(groups)]

        more = list(lax.cond(info[0, DEEP] > usual, deep, flat))
    before.clear()
    starts = list(range(0, usual, GROUP))
    held = [group_of(s, more if s == starts[-1] and more else None) for s in starts]
    held += [more[i:i + groups] for i in range(0, len(more), groups)]
    near = [h[x] for x in range(groups // 2) for h in held]
    far = [h[x] for x in range(groups // 2, groups) for h in held]
    pieces = turn(route, info, near, far, rows_split)
    direct = direct_rows(route, near, far)
    got = [pieces[0]] + [along(pieces[s], s) for s in range(1, rows_split)]
    return direct, join(info, got).transpose(1, 0, 2)


def rank_table(labels, groups, slots_per):
    total_rows = labels.shape[0]
    member = (labels[None, :] == jnp.arange(groups, dtype=jnp.int32)[:, None]).astype(jnp.int32)
    before = jnp.cumsum(member, axis=1) - 1
    placed = member[:, None, :] * (
        before[:, None, :] == jnp.arange(slots_per, dtype=jnp.int32)[None, :, None]
    ).astype(jnp.int32)
    numbers = jnp.arange(total_rows, dtype=jnp.int32) + 1
    return jnp.sum(placed * numbers[None, None, :], axis=2) - 1


def whole_pair(val_first, val_second, con_first, con_second, screen_rows):
    val_count = val_first.shape[0]
    con_count = con_first.shape[0]
    val_pairs = val_first[:, None, :].astype(jnp.float32) * val_second[None, :, :].astype(
        jnp.float32
    )
    val_pairs = val_pairs.reshape(val_count * val_count, val_first.shape[1]).astype(jnp.bfloat16)
    con_pairs = con_first[:, None, :].astype(jnp.float32) * con_second[None, :, :].astype(
        jnp.float32
    )
    con_pairs = con_pairs.reshape(con_count * con_count, con_first.shape[1]).astype(jnp.bfloat16)
    interim = lax.dot_general(
        screen_rows, con_pairs, (((1,), (1,)), ((), ())), preferred_element_type=jnp.float32
    ).astype(jnp.bfloat16)
    partial_sum = jnp.dot(val_pairs, interim, preferred_element_type=jnp.float32)
    partial_sum = partial_sum.reshape(val_count, val_count, con_count, con_count).transpose(
        0, 2, 1, 3
    )
    return partial_sum.reshape(val_count * con_count, val_count * con_count)


def plain_shards(valence_bands, conduction_bands, screened, pair_list, transfer_index, owner_map):
    groups = lax.axis_size("pb")
    rows_split = lax.axis_size("row")
    device = lax.axis_index("pb")
    val_all, con_local = (
        lax.all_gather(valence_bands, "pb", axis=0, tiled=True),
        lax.all_gather(conduction_bands, "pb", axis=0, tiled=True),
    )
    slot_table = rank_table(transfer_index[:, 0], groups, MOST)
    own_slots = lax.dynamic_index_in_dim(slot_table, device, 0, keepdims=False)
    live_pair = jnp.maximum(own_slots, 0)
    slot_first = jnp.take(owner_map, jnp.take(pair_list[:, 0], live_pair))
    slot_second = jnp.take(owner_map, jnp.take(pair_list[:, 1], live_pair))
    val_first = jnp.take(val_all, slot_first, axis=0)
    val_second = jnp.take(val_all, slot_second, axis=0)
    con_full = lax.all_gather(con_local, "row", axis=2, tiled=True)
    con_first = jnp.take(con_full, slot_first, axis=0)
    con_second = jnp.take(con_full, slot_second, axis=0)
    screen_rows = screened[0]

    def one_slot(operands):
        return whole_pair(operands[0], operands[1], operands[2], operands[3], screen_rows)

    partials = lax.map(one_slot, (val_first, val_second, con_first, con_second))
    shares = lax.psum_scatter(partials, "row", scatter_dimension=1, tiled=True).astype(jnp.bfloat16)
    band_rows = shares.shape[1]
    mirror_table = rank_table(jnp.take(owner_map, pair_list[:, 1]), groups, PAIR_DEV)
    flat_slots = slot_table.reshape(-1)
    own_direct = device * PAIR_DEV + jnp.arange(PAIR_DEV, dtype=jnp.int32)
    own_mirror = lax.dynamic_index_in_dim(mirror_table, device, 0, keepdims=False)
    wanted = jnp.concatenate([own_direct, own_mirror])
    select = (wanted[:, None] == flat_slots[None, :]).astype(jnp.bfloat16)
    arrived = jnp.einsum(
        "ji,ixy->jxy",
        select,
        lax.all_gather(shares, "pb", axis=0, tiled=True),
        preferred_element_type=jnp.float32,
    )
    direct = arrived[:PAIR_DEV].astype(jnp.bfloat16)
    mirror_rows = arrived[PAIR_DEV:].astype(jnp.bfloat16)
    turned = jnp.transpose(mirror_rows, (0, 2, 1)).reshape(
        PAIR_DEV, rows_split, band_rows, band_rows
    )
    swapped = lax.all_to_all(turned, "row", split_axis=1, concat_axis=3, tiled=True)
    mirror = swapped.reshape(PAIR_DEV, band_rows, band_rows * rows_split)
    return (direct, mirror)


def solution(mesh):
    in_specs = (P("pb", None, "row"), P("pb", None, "row"), P("pb", "row", None), P(), P(), P())
    out_specs = (P("pb", "row", None), P("pb", "row", None))

    def step(valence_bands, conduction_bands, *rest):
        groups, rows_split = mesh.shape["pb"], mesh.shape["row"]
        nv, nc = valence_bands.shape[1], conduction_bands.shape[1]
        even = nv == nc and nv % rows_split == 0 and groups & (groups - 1) == 0 and rows_split & (rows_split - 1) == 0 and groups >= 4
        body = shards if even else plain_shards

        mapped = jax.shard_map(body, mesh=mesh, in_specs=in_specs, out_specs=out_specs, check_vma=False)
        return mapped(valence_bands, conduction_bands, *rest)

    return step
```

```python
import functools
import math

import jax
import jax.numpy as jnp
from jax import lax
from jax.experimental import pallas as pl
from jax.experimental.pallas import tpu as pltpu
from jax.sharding import PartitionSpec as P


PAIR_DEV = 2
MOST = 6
SUB = 8
F32, BF16, I32 = jnp.float32, jnp.bfloat16, jnp.int32
SMEM = pl.BlockSpec(memory_space=pltpu.SMEM)
VMEM = pl.BlockSpec(memory_space=pltpu.VMEM)
ANY = pl.BlockSpec(memory_space=pl.ANY)
LIVE, SWAP, FBIT, FIDX, SBIT, SIDX, ROW, DEEP = range(8)
GROUP = 2


def table_body(pairs, transfers, owners, slots_out, route_out, rank, count, *, slots, groups, rows_split):
    me = lax.axis_index("pb")
    row = lax.axis_index("row")
    total = pairs.shape[1]
    partner = me ^ 1
    for q in range(groups):
        count[q] = 0
    for p in range(total):
        q = transfers[p]
        rank[p] = count[q]
        count[q] = count[q] + 1
    for s in range(slots):
        for k in range(8):
            slots_out[s, k] = 0
        slots_out[s, ROW] = row
    deep = 0
    for q in range(0, groups, 2):
        deep = jnp.maximum(deep, (count[q] + count[q + 1] + 1) // 2)
    for s in range(slots):
        slots_out[s, DEEP] = deep

    def place(p):
        q = transfers[p]
        low = q & ~1
        pos = rank[p] + jnp.where(q == low, 0, count[low])
        half = (count[low] + count[low + 1] + 1) // 2
        core = (pos >= half).astype(I32)
        return q, low | core, pos - core * half

    wanted = {}
    for d, name in ((me, 0), (partner, 1)):
        for j in range(PAIR_DEV):
            wanted[name, j] = d * PAIR_DEV + j

    def put(name, t, p):
        _, source, slot = place(p)
        away = source ^ jnp.where(name == 0, me, partner)
        route_out[name, t, 0] = away & 1
        route_out[name, t, 1] = (away >> 1) * (-(-slots // GROUP) * GROUP) + slot

    for name in range(2):
        for j in range(PAIR_DEV):
            put(name, j, wanted[name, j])
    for k in range(2):
        count[groups + k] = 0
    for p in range(total):
        q, source, slot = place(p)
        first = owners[pairs[0, p]] ^ me
        second = owners[pairs[1, p]] ^ me

        @pl.when(source == me)
        def _(q=q, slot=slot, first=first, second=second):
            slots_out[slot, LIVE] = 1
            slots_out[slot, SWAP] = (q != me).astype(I32)
            slots_out[slot, FBIT] = first & 1
            slots_out[slot, FIDX] = first >> 1
            slots_out[slot, SBIT] = second & 1
            slots_out[slot, SIDX] = second >> 1

        for name, d in ((0, 0), (1, 1)):
            @pl.when(second == d)
            def _(name=name, p=p):
                k = count[groups + name]
                put(name, PAIR_DEV + k, p)
                count[groups + name] = k + 1


def tables(pair_list, transfer_index, owner_map, slots, groups, rows_split):
    body = functools.partial(table_body, slots=slots, groups=groups, rows_split=rows_split)
    return pl.pallas_call(
        body,
        out_shape=[
            jax.ShapeDtypeStruct((slots, 8), I32),
            jax.ShapeDtypeStruct((2, 2 * PAIR_DEV, 2), I32),
        ],
        in_specs=[SMEM] * 3,
        out_specs=[SMEM] * 2,
        scratch_shapes=[pltpu.SMEM((pair_list.shape[0],), I32), pltpu.SMEM((groups + 2,), I32)],
    )(pair_list.T, transfer_index.reshape(-1), owner_map)


def pair_body(info, own, own_rest, other, other_rest, w_own, w_other, *rest, slots, rows_split, parts, chunk):
    outs = rest[:rows_split]
    near, far, products, wbuf, interim, val_products, result, sem, con_sem = rest[rows_split:]
    nc = own.shape[1] // 2
    nloc = own.shape[2]
    m = w_own.shape[0]
    nv = nc
    per = nv // rows_split
    height = val_products.shape[0] // rows_split
    step = m // parts
    base = slots[0]
    row = info[base, ROW]

    def band_copies(i, which, bit):
        k = info[base + i, FIDX if which == 0 else SIDX]
        src, src_rest = (own, own_rest) if bit == 0 else (other, other_rest)
        return (
            pltpu.make_async_copy(src.at[k], near.at[i, which], con_sem.at[0, i, which]),
            pltpu.make_async_copy(src_rest.at[k], far.at[i, which], con_sem.at[1, i, which]),
        )

    def w_copy(which, k):
        rows = pl.ds(k * step, step)
        return pltpu.make_async_copy((w_own, w_other)[which].at[rows], wbuf.at[which, rows], sem.at[which, k])

    count = len(slots)
    live = [info[s, LIVE] != 0 for s in slots]
    for i in range(count):
        for which, flag in ((0, FBIT), (1, SBIT)):
            for bit in range(2):
                @pl.when(live[i] & (info[slots[i], flag] == bit))
                def _(i=i, which=which, bit=bit):
                    for c in band_copies(i, which, bit):
                        c.start()
        for which in range(2):
            new = live[i] & (info[slots[i], SWAP] == which)
            for before in range(i):
                new = new & ~(live[before] & (info[slots[before], SWAP] == which))

            @pl.when(new)
            def _(which=which):
                for k in range(parts):
                    w_copy(which, k).start()

    def lows(n):
        rows = lax.broadcasted_iota(I32, (SUB, n), 0)
        return {i: rows < i for i in range(1, SUB)}

    def tile(lines, tiled, at, total, width, low):
        n = tiled.shape[1]
        lo, hi = min(at, total - 1) // width, min(at + SUB - 1, total - 1) // width
        left = jnp.broadcast_to(lines[lo:lo + 1], (SUB, n))
        if hi != lo:
            left = jnp.where(low[hi * width - at], left, jnp.broadcast_to(lines[hi:hi + 1], (SUB, n)))
        start = at % tiled.shape[0]
        return left * tiled[start:start + SUB]

    group = 2 * SUB // math.gcd(nc, 2 * SUB)

    @pl.loop(0, count)
    def _(i):
        slot = base + i

        @pl.when(info[slot, LIVE] != 0)
        def _():
            for which in range(2):
                pltpu.make_async_copy(own.at[0], near.at[i, which], con_sem.at[0, i, which]).wait()
                pltpu.make_async_copy(own_rest.at[0], far.at[i, which], con_sem.at[1, i, which]).wait()
            low = lows(chunk)
            for j in range(rows_split):
                block = row ^ j
                for k in range(0, nloc, chunk):
                    def band(which):
                        if j == 0:
                            return near[i, which, :, k:k + chunk].astype(F32)[:nc]
                        return far[i, which, :, k:k + chunk].astype(F32)[(j - 1) * nc:j * nc]

                    lines = band(0)
                    tiled = jnp.concatenate([band(1)] * group, axis=0)
                    cols = pl.ds(pl.multiple_of(block * nloc + k, 128), chunk)
                    for at in range(0, nc * nc, 2 * SUB):
                        two = [tile(lines, tiled, at + o, nc * nc, nc, low) for o in (0, SUB)]
                        products[at:at + 2 * SUB, cols] = jnp.concatenate(two, axis=0).astype(BF16)

            low = lows(nloc)
            lines = near[i, 0].astype(F32)[nc:]
            tiled = jnp.concatenate([near[i, 1].astype(F32)[nc:]] * (per + 1), axis=0)
            for s in range(rows_split):
                for at in range(0, height, SUB):
                    x = tile(lines[s * per:(s + 1) * per], tiled, at, per * nv, nv, low)
                    val_products[s * height + at:s * height + at + SUB, :] = x.astype(BF16)

            swap = info[slot, SWAP]
            fresh = jnp.bool_(True)
            for before in range(count):
                used = live[before] & (info[slots[before], SWAP] == swap) & (before < i)
                fresh = fresh & ~used
            for k in range(parts):
                for which in range(2):
                    @pl.when(fresh & (swap == which))
                    def _(which=which, k=k):
                        w_copy(which, k).wait()
                got = lax.dot_general(
                    products[...], wbuf[swap, k * step:(k + 1) * step, :], (((1,), (1,)), ((), ())),
                    preferred_element_type=F32,
                )
                interim[:, k * step:(k + 1) * step] = got.astype(BF16)
            res = lax.dot_general(
                val_products[...], interim[...], (((1,), (1,)), ((), ())), preferred_element_type=F32
            )
            for s in range(rows_split):
                result[s] = res[s * height:(s + 1) * height]
            for g in range(count):
                @pl.when(i == g)
                def _(g=g):
                    for s in range(rows_split):
                        piece = result[row ^ s]
                        outs[s][:, g * nc * nc:(g + 1) * nc * nc] = piece[:per * nv].astype(BF16)


def pair_call(info, slots, own, own_rest, other, other_rest, w_own, w_other, rows_split, parts=2, chunk=256):
    nc = own.shape[1] // 2
    m, n = w_own.shape
    nv = nc
    per = nv // rows_split
    height = -(-per * nv // SUB) * SUB
    count = len(slots)
    return pl.pallas_call(
        functools.partial(pair_body, slots=slots, rows_split=rows_split, parts=parts, chunk=chunk),
        out_shape=[jax.ShapeDtypeStruct((per * nv, count * nc * nc), BF16)] * rows_split,
        in_specs=[SMEM] + [ANY] * 6,
        out_specs=[VMEM] * rows_split,
        scratch_shapes=[
            pltpu.VMEM((count, 2) + own.shape[1:], BF16),
            pltpu.VMEM((count, 2) + own_rest.shape[1:], BF16),
            pltpu.VMEM((nc * nc, n), BF16),
            pltpu.VMEM((2, m, n), BF16),
            pltpu.VMEM((nc * nc, m), BF16),
            pltpu.VMEM((rows_split * height, m), BF16),
            pltpu.VMEM((rows_split, height, nc * nc), F32),
            pltpu.SemaphoreType.DMA((2, parts)),
            pltpu.SemaphoreType.DMA((2, count, 2)),
        ],
        compiler_params=pltpu.CompilerParams(vmem_limit_bytes=60 << 20),
        cost_estimate=pl.CostEstimate(
            flops=2 * count * nc * nc * m * n, bytes_accessed=2 * m * n, transcendentals=0
        ),
    )(info, own, own_rest, other, other_rest, w_own, w_other)


def fetch(route, near, far, held, sem, wants):
    for i, t in enumerate(wants):
        code = route[0, t, 1]
        for bit, blocks in ((0, near), (1, far)):
            @pl.when(route[0, t, 0] == bit)
            def _(i=i, code=code, blocks=blocks):
                for k, block in enumerate(blocks):
                    @pl.when(code // GROUP == k)
                    def _(block=block):
                        pltpu.make_async_copy(block.at[code % GROUP], held.at[i], sem.at[i]).start()
    for i in range(len(wants)):
        pltpu.make_async_copy(near[0].at[0], held.at[i], sem.at[i]).wait()


def direct_body(route, *rest):
    blocks, direct, sem = rest[:-2], rest[-2], rest[-1]
    half = len(blocks) // 2
    fetch(route, blocks[:half], blocks[half:], direct, sem, range(PAIR_DEV))


def direct_rows(route, near, far):
    return pl.pallas_call(
        direct_body,
        out_shape=jax.ShapeDtypeStruct((PAIR_DEV,) + near[0].shape[1:], BF16),
        in_specs=[SMEM] + [ANY] * (2 * len(near)),
        out_specs=VMEM,
        scratch_shapes=[pltpu.SemaphoreType.DMA((PAIR_DEV,))],
    )(route, *near, *far)


def turn_body(route, info, *rest, rows_split):
    blocks, outs = rest[:-(rows_split + 3)], rest[-(rows_split + 3):-3]
    held, turned, sem = rest[-3:]
    half = len(blocks) // 2
    fetch(route, blocks[:half], blocks[half:], held, sem, range(PAIR_DEV, 2 * PAIR_DEV))
    row = info[0, ROW]
    width = turned.shape[2]
    for t in range(PAIR_DEV):
        x = held[t].astype(F32).T
        for s in range(rows_split):
            turned[t, s] = x[s * width:(s + 1) * width]
    for s in range(rows_split):
        for t in range(PAIR_DEV):
            outs[s][t] = turned[t, row ^ s].astype(BF16)


def turn(route, info, near, far, rows_split):
    rows, columns = near[0].shape[1:]
    width = columns // rows_split
    return pl.pallas_call(
        functools.partial(turn_body, rows_split=rows_split),
        out_shape=[jax.ShapeDtypeStruct((PAIR_DEV, width, rows), BF16)] * rows_split,
        in_specs=[SMEM, SMEM] + [ANY] * (2 * len(near)),
        out_specs=[VMEM] * rows_split,
        scratch_shapes=[
            pltpu.VMEM((PAIR_DEV, rows, columns), BF16),
            pltpu.VMEM((PAIR_DEV, rows_split, width, rows), F32),
            pltpu.SemaphoreType.DMA((PAIR_DEV,)),
        ],
    )(route, info, *near, *far)


def join_body(info, *rest, rows_split):
    pieces, mirror, placed = rest[:rows_split], rest[rows_split], rest[rows_split + 1]
    row = info[0, ROW]
    for s in range(rows_split):
        for t in range(PAIR_DEV):
            placed[t, row ^ s] = pieces[s][t].astype(F32)
    whole = [jnp.concatenate([placed[t, s] for s in range(rows_split)], axis=1) for t in range(PAIR_DEV)]
    mirror[...] = jnp.stack(whole, axis=1).astype(BF16)


def join(info, pieces):
    rows_split = len(pieces)
    _, height, width = pieces[0].shape
    return pl.pallas_call(
        functools.partial(join_body, rows_split=rows_split),
        out_shape=jax.ShapeDtypeStruct((height, PAIR_DEV, width * rows_split), BF16),
        in_specs=[SMEM] + [VMEM] * rows_split,
        out_specs=VMEM,
        scratch_shapes=[pltpu.VMEM((PAIR_DEV, rows_split, height, width), F32)],
    )(info, *pieces)


def shards(valence_bands, conduction_bands, screened, pair_list, transfer_index, owner_map):
    groups = lax.axis_size("pb")
    rows_split = lax.axis_size("row")
    total = pair_list.shape[0]
    slots = -(-min(2 * MOST, total - (groups - 2)) // 2)
    nc, nv = conduction_bands.shape[1], valence_bands.shape[1]
    per = nv // rows_split

    def away(x, k):
        return lax.ppermute(x, "pb", [(i, i ^ k) for i in range(groups)])

    def along(x, k):
        return lax.ppermute(x, "row", [(i, i ^ k) for i in range(rows_split)])

    w_own = screened[0]
    w_other = away(w_own, 1)
    bands = jnp.concatenate([conduction_bands[0], valence_bands[0]], axis=0)
    con = []
    for s in range(1, rows_split):
        con.append(along(conduction_bands[0], s))
    info, route = tables(pair_list, transfer_index, owner_map, slots, groups, rows_split)
    own = [bands]
    for k in range(1, groups // 2):
        own.append(away(bands, 2 * k))
    own = jnp.stack(own)
    con_rest = jnp.concatenate(con, axis=0)
    con_rest, info, route = lax.optimization_barrier((con_rest, info, route))
    own_rest = [con_rest]
    for k in range(1, groups // 2):
        own_rest.append(away(con_rest, 2 * k))
    own_rest = jnp.stack(own_rest)
    other = away(own, 1)
    other_rest = away(own_rest, 1)

    before = []

    def some_slots(which, early=None):
        table = info
        if before:
            table, _ = lax.optimization_barrier((info, before[-1]))
        pieces = pair_call(table, which, own, own_rest, other, other_rest, w_own, w_other, rows_split)
        before.append(pieces[0])
        shares = [pieces[0]]
        for s in range(1, rows_split):
            shares.append(along(pieces[s], s))
        if early is not None:
            shares, early[:] = lax.optimization_barrier((shares, list(early)))
        return functools.reduce(lambda a, b: a + b, [x.astype(F32) for x in shares]).astype(BF16)

    def spread(summed, count):
        x = summed.reshape(per, nv, count, nc, nc).transpose(2, 0, 3, 1, 4).reshape(count, per * nc, nv * nc)
        out = [x]
        for k in range(1, groups // 2):
            out.append(away(x, 2 * k))
        return out + [away(x, 1) for x in out]

    def group_of(s, early=None):
        which = tuple(range(s, min(s + GROUP, slots)))
        return spread(some_slots(which, early), len(which))

    usual = min(slots, 2 * GROUP)
    more = []
    if slots > usual:
        shape = (per * nc, nv * nc)

        def deep():
            before.clear()
            more = [group_of(s) for s in range(usual, slots, GROUP)]
            return [x for m in more for x in m]

        def flat():
            counts = [min(GROUP, slots - s) for s in range(usual, slots, GROUP)]
            return [jnp.zeros((count,) + shape, BF16) for count in counts for _ in range(groups)]

        more = list(lax.cond(info[0, DEEP] > usual, deep, flat))
    before.clear()
    starts = list(range(0, usual, GROUP))
    held = [group_of(s, more if s == starts[-1] and more else None) for s in starts]
    held += [more[i:i + groups] for i in range(0, len(more), groups)]
    near = [h[x] for x in range(groups // 2) for h in held]
    far = [h[x] for x in range(groups // 2, groups) for h in held]
    pieces = turn(route, info, near, far, rows_split)
    direct = direct_rows(route, near, far)
    got = [pieces[0]] + [along(pieces[s], s) for s in range(1, rows_split)]
    return direct, join(info, got).transpose(1, 0, 2)


def rank_table(labels, groups, slots_per):
    total_rows = labels.shape[0]
    member = (labels[None, :] == jnp.arange(groups, dtype=jnp.int32)[:, None]).astype(jnp.int32)
    before = jnp.cumsum(member, axis=1) - 1
    placed = member[:, None, :] * (
        before[:, None, :] == jnp.arange(slots_per, dtype=jnp.int32)[None, :, None]
    ).astype(jnp.int32)
    numbers = jnp.arange(total_rows, dtype=jnp.int32) + 1
    return jnp.sum(placed * numbers[None, None, :], axis=2) - 1


def whole_pair(val_first, val_second, con_first, con_second, screen_rows):
    val_count = val_first.shape[0]
    con_count = con_first.shape[0]
    val_pairs = val_first[:, None, :].astype(jnp.float32) * val_second[None, :, :].astype(
        jnp.float32
    )
    val_pairs = val_pairs.reshape(val_count * val_count, val_first.shape[1]).astype(jnp.bfloat16)
    con_pairs = con_first[:, None, :].astype(jnp.float32) * con_second[None, :, :].astype(
        jnp.float32
    )
    con_pairs = con_pairs.reshape(con_count * con_count, con_first.shape[1]).astype(jnp.bfloat16)
    interim = lax.dot_general(
        screen_rows, con_pairs, (((1,), (1,)), ((), ())), preferred_element_type=jnp.float32
    ).astype(jnp.bfloat16)
    partial_sum = jnp.dot(val_pairs, interim, preferred_element_type=jnp.float32)
    partial_sum = partial_sum.reshape(val_count, val_count, con_count, con_count).transpose(
        0, 2, 1, 3
    )
    return partial_sum.reshape(val_count * con_count, val_count * con_count)


def plain_shards(valence_bands, conduction_bands, screened, pair_list, transfer_index, owner_map):
    groups = lax.axis_size("pb")
    rows_split = lax.axis_size("row")
    device = lax.axis_index("pb")
    val_all, con_local = (
        lax.all_gather(valence_bands, "pb", axis=0, tiled=True),
        lax.all_gather(conduction_bands, "pb", axis=0, tiled=True),
    )
    slot_table = rank_table(transfer_index[:, 0], groups, MOST)
    own_slots = lax.dynamic_index_in_dim(slot_table, device, 0, keepdims=False)
    live_pair = jnp.maximum(own_slots, 0)
    slot_first = jnp.take(owner_map, jnp.take(pair_list[:, 0], live_pair))
    slot_second = jnp.take(owner_map, jnp.take(pair_list[:, 1], live_pair))
    val_first = jnp.take(val_all, slot_first, axis=0)
    val_second = jnp.take(val_all, slot_second, axis=0)
    con_full = lax.all_gather(con_local, "row", axis=2, tiled=True)
    con_first = jnp.take(con_full, slot_first, axis=0)
    con_second = jnp.take(con_full, slot_second, axis=0)
    screen_rows = screened[0]

    def one_slot(operands):
        return whole_pair(operands[0], operands[1], operands[2], operands[3], screen_rows)

    partials = lax.map(one_slot, (val_first, val_second, con_first, con_second))
    shares = lax.psum_scatter(partials, "row", scatter_dimension=1, tiled=True).astype(jnp.bfloat16)
    band_rows = shares.shape[1]
    mirror_table = rank_table(jnp.take(owner_map, pair_list[:, 1]), groups, PAIR_DEV)
    flat_slots = slot_table.reshape(-1)
    own_direct = device * PAIR_DEV + jnp.arange(PAIR_DEV, dtype=jnp.int32)
    own_mirror = lax.dynamic_index_in_dim(mirror_table, device, 0, keepdims=False)
    wanted = jnp.concatenate([own_direct, own_mirror])
    select = (wanted[:, None] == flat_slots[None, :]).astype(jnp.bfloat16)
    arrived = jnp.einsum(
        "ji,ixy->jxy",
        select,
        lax.all_gather(shares, "pb", axis=0, tiled=True),
        preferred_element_type=jnp.float32,
    )
    direct = arrived[:PAIR_DEV].astype(jnp.bfloat16)
    mirror_rows = arrived[PAIR_DEV:].astype(jnp.bfloat16)
    turned = jnp.transpose(mirror_rows, (0, 2, 1)).reshape(
        PAIR_DEV, rows_split, band_rows, band_rows
    )
    swapped = lax.all_to_all(turned, "row", split_axis=1, concat_axis=3, tiled=True)
    mirror = swapped.reshape(PAIR_DEV, band_rows, band_rows * rows_split)
    return (direct, mirror)


def solution(mesh):
    in_specs = (P("pb", None, "row"), P("pb", None, "row"), P("pb", "row", None), P(), P(), P())
    out_specs = (P("pb", "row", None), P("pb", "row", None))

    def step(valence_bands, conduction_bands, *rest):
        groups, rows_split = mesh.shape["pb"], mesh.shape["row"]
        nv, nc = valence_bands.shape[1], conduction_bands.shape[1]
        even = nv == nc and nv % rows_split == 0 and groups & (groups - 1) == 0 and rows_split & (rows_split - 1) == 0 and groups >= 4
        body = shards if even else plain_shards

        mapped = jax.shard_map(body, mesh=mesh, in_specs=in_specs, out_specs=out_specs, check_vma=False)
        return mapped(valence_bands, conduction_bands, *rest)

    return step
```
